128 devices in a mesh: src: 8 (over y_lo, x), tgt: 16 (over z, y_hi, core).
Axes of the slice: x: 4, y: 4 (y_hi: 2, y_lo: 2; y = y_hi * 2 + y_lo), z: 4, core: 2. Of those that a mesh axis runs over, the one named last changes fastest.
Arguments:
- residual: bfloat16 [4, 512, 2304], replicated, may hold values from -6 to 6
- targets: bfloat16 [4, 2304, 512], P(None, 'tgt'), may hold values from -6 to 6
- enc_weight: bfloat16 [4, 2304, 16384], P(None, None, ('src', 'tgt')), may hold values from -0.125 to 0.125
- enc_bias: float32 [4, 16384], P(None, ('src', 'tgt')), may hold values from -3 to 3
- active: int32 [4, 512, 16384], P(None, None, ('src', 'tgt')), may hold values 0 or 1
- dec_weight: bfloat16 [80, 2304, 2048], P('src', 'tgt'), may hold values from -0.046875 to 0.046875
- dec_bias: float32 [4, 2304], P(None, 'tgt'), may hold values from -3 to 3
- tile_pairs: int32 [80, 2], P('src'), may hold values from 0 to 3, as said below
Outputs:
- dec_grad: bfloat16 [80, 2304, 2048], P('src', 'tgt')
- enc_grad: bfloat16 [4, 2304, 16384], P(None, None, ('src', 'tgt'))
- bias_grad: float32 [4, 16384], P(None, ('src', 'tgt'))
The draws below stay inside these ranges and needn't reach their ends.
Inputs may be any that keep to these rules, and one draw needn't show every extreme that they name: `tile_pairs`: rows b * 10 to (b + 1) * 10 - 1 serve latent block b; among them each pair (source, target) with source <= target appears exactly once, source in column 0 and target in column 1.
All inputs are finite; a program needn't handle non-finite values. No bound on the sum of `active` on one device may be relied on, other than what follows from the above.
Results may differ from the reference program's by a relative error of at most 0.019.
Values may be sent and summed in bfloat16 or wider, within the bound.
A program may use at most 128 MiB of HBM per device.

```python
import jax
import jax.numpy as jnp
import numpy as np
from jax import lax

D = 2304
F = 16384
LAYERS = 4
TOK = 512
PAIRS = 10
ROWS = 80
BLOCK = 2048


def shuffle_pairs(subkey):
    return jax.random.permutation(subkey, PAIRS)


def draw_tile_pairs(key, part):
    listing = []
    for source in range(LAYERS):
        for target in range(source, LAYERS):
            listing.append((source, target))
    table = jnp.asarray(np.array(listing, dtype=np.int32))
    block_count = ROWS // PAIRS
    subkeys = jax.random.split(jax.random.fold_in(key, 11), block_count)
    orders = jax.vmap(shuffle_pairs)(subkeys)
    return table[orders.reshape(-1)].astype(jnp.int32)


def plant(values, stream_key, least, top_value):
    shape = values.shape
    place = [jax.random.randint(jax.random.fold_in(stream_key, axis), (), 0, shape[axis]) for axis in range(len(shape))]
    values = values.at[tuple(place)].set(least)
    longest = shape.index(max(shape))
    place[longest] = (place[longest] + 1) % shape[longest]
    return values.at[tuple(place)].set(top_value)


def block_levels(key, extent, shards, least, top_value):
    loudness, own = 1.0, jax.random.fold_in(key, 6)
    for dim, blocks in shards:
        steps = jnp.exp(jax.random.uniform(jax.random.fold_in(own, dim), (blocks,), jnp.float32, least / len(shards), top_value / len(shards)))
        loudness = loudness * jnp.repeat(steps, extent[dim] // blocks).reshape([-1 if axis == dim else 1 for axis in range(len(extent))])
    return loudness


def normal_values(rng, extent, deviation, reach, cuts=(), held_as=jnp.bfloat16):
    loudness = block_levels(rng, extent, cuts, -0.22, 0.18) if cuts else 1.0
    values = jax.random.normal(rng, extent, jnp.float32) * deviation * loudness
    return jnp.minimum(jnp.maximum(values, -reach), reach).astype(held_as)


def setup_inputs(seed: int = 0) -> dict:
    splits = jax.random.split(jax.random.key(seed), 9)
    residual = normal_values(splits[0], (LAYERS, TOK, D), 1.0, 6.0)
    targets = normal_values(splits[1], (LAYERS, D, TOK), 1.0, 6.0, ((1, 16),))
    enc_weight = normal_values(splits[2], (LAYERS, D, F), D ** -0.5, 0.125, ((2, 128),))
    enc_bias = normal_values(splits[3], (LAYERS, F), 0.5, 3.0, ((1, 128),), jnp.float32)
    active = plant((jax.random.randint(splits[4], (LAYERS, TOK, F), 0, 3) < 1).astype(jnp.int32), jax.random.fold_in(splits[4], 1), 0, 1)
    dec_weight = normal_values(splits[5], (ROWS, D, BLOCK), (F * LAYERS // 4) ** -0.5, 0.046875, ((0, 8), (1, 16)))
    dec_bias = normal_values(splits[6], (LAYERS, D), 0.5, 3.0, ((1, 16),), jnp.float32)
    tile_pairs = draw_tile_pairs(jax.random.fold_in(splits[8], 71), 0)
    return {"residual": residual, "targets": targets, "enc_weight": enc_weight, "enc_bias": enc_bias, "active": active, "dec_weight": dec_weight, "dec_bias": dec_bias, "tile_pairs": tile_pairs}


def add_layer(total, index, value):
    current = lax.dynamic_slice_in_dim(total, index, 1, 0)
    return lax.dynamic_update_slice_in_dim(total, current + value[None], index, 0)


def latent_block(latent, source, block_start, block_width):
    layer_rows = lax.dynamic_index_in_dim(latent, source, 0, keepdims=False)
    return lax.dynamic_slice_in_dim(layer_rows, block_start, block_width, 1)


def reference(residual, targets, enc_weight, enc_bias, active, dec_weight, dec_bias, tile_pairs):
    layers = residual.shape[0]
    tok_all = residual.shape[1]
    model_width = residual.shape[2]
    latents = enc_weight.shape[2]
    block_width = dec_weight.shape[2]
    mask_full = active.astype(jnp.float32)
    preact = jnp.einsum("lrd,ldf->lrf", residual.astype(jnp.float32), enc_weight.astype(jnp.float32))
    latent = ((preact + enc_bias[:, None, :]) * mask_full).astype(jnp.bfloat16)
    source_ids = tile_pairs[:, 0].astype(jnp.int32)
    target_ids = tile_pairs[:, 1].astype(jnp.int32)
    row_ids = jnp.arange(tile_pairs.shape[0], dtype=jnp.int32)
    block_starts = ((row_ids // PAIRS) * block_width).astype(jnp.int32)

    def rebuild(recon_sum, slot_data):
        weight, source, target, block_start = slot_data
        lat_block = latent_block(latent, source, block_start, block_width)
        recon_term = lax.dot_general(weight, lat_block, (((1,), (1,)), ((), ())), preferred_element_type=jnp.float32)
        return add_layer(recon_sum, target, recon_term), None

    recon_zero = jnp.zeros((layers, model_width, tok_all), jnp.float32)
    recon = lax.scan(rebuild, recon_zero, (dec_weight, source_ids, target_ids, block_starts))[0]
    recon = recon + dec_bias[:, :, None]
    error_full = (recon - targets.astype(jnp.float32)).astype(jnp.bfloat16)
    zero_index = jnp.zeros((), jnp.int32)

    def backward(grad_sum, slot_data):
        weight, source, target, block_start = slot_data
        error_rows = lax.dynamic_index_in_dim(error_full, target, 0, keepdims=False)
        lat_block = latent_block(latent, source, block_start, block_width)
        dec_term = lax.dot_general(error_rows, lat_block, (((1,), (0,)), ((), ())), preferred_element_type=jnp.float32)
        lat_term = lax.dot_general(error_rows, weight, (((0,), (0,)), ((), ())), preferred_element_type=jnp.float32)
        current = lax.dynamic_slice(grad_sum, (source, zero_index, block_start), (1, tok_all, block_width))
        grad_sum = lax.dynamic_update_slice(grad_sum, current + lat_term[None], (source, zero_index, block_start))
        return grad_sum, dec_term.astype(jnp.bfloat16)

    grad_zero = jnp.zeros((layers, tok_all, latents), jnp.float32)
    grad_sum, dec_grad = lax.scan(backward, grad_zero, (dec_weight, source_ids, target_ids, block_starts))
    pre_grad = (grad_sum * mask_full).astype(jnp.bfloat16)
    enc_grad = jnp.einsum("lrd,lrf->ldf", residual.astype(jnp.float32), pre_grad.astype(jnp.float32)).astype(jnp.bfloat16)
    bias_grad = jnp.sum(pre_grad.astype(jnp.float32), axis=1)
    return (dec_grad, enc_grad, bias_grad)
```

```python
import functools

import jax
import jax.numpy as jnp
from jax import lax
from jax.experimental import pallas as pl
from jax.experimental.pallas import tpu as pltpu
from jax.sharding import PartitionSpec as P

MESH = pl.DeviceIdType.MESH
F32 = jnp.float32
BF16 = jnp.bfloat16
LAYERS = 4
HALVES = 2
ITEMS = LAYERS * HALVES
A_Y, A_OWN_UP, A_OWN_DOWN, A_PAIR_UP, A_PAIR_DOWN, A_FWD_UP, A_FWD_DOWN, A_TWIN = range(8)
R_TWIN, R_RELAY_UP, R_RELAY_DOWN, R_LAST_UP, R_LAST_DOWN, R_Y = range(6)


def column_of(row, size):
    down = lax.broadcasted_iota(jnp.int32, (size, size), 0)
    across = lax.broadcasted_iota(jnp.int32, (size, size), 1)
    spread = jnp.where(down == across, jnp.broadcast_to(row, (size, size)), 0.0)
    return jnp.sum(spread, axis=1, keepdims=True)


def kernel(
    res_hbm, tgt_hbm, encw_hbm, encb_ref, act_hbm, decw_hbm, decb_ref, pairs_ref,
    dec_hbm, enc_hbm, bias_ref,
    res_v, tgt_v, encw_v, act_v, w_v, lat_v, p_acc, p_snd, p_rcv, err_v, g_v, tw_v, s_v,
    zr_v, zf_v, ty_v, yr_v, pre_v, dst_v, eo_v, row_s,
    res_sem, encw_sem, act_sem, w_sem, tgt_sem, dst_sem, eo_sem,
    a_send, a_recv, r_send, r_recv, p_send, p_recv, e_send, e_recv,
):
    tok = res_v.shape[1]
    chunk = tok // HALVES
    part = chunk // 2
    feats = w_v.shape[1]
    width = res_v.shape[2]

    src = lax.axis_index("src")
    tgt = lax.axis_index("tgt")
    x, yl = lax.rem(src, 4), src // 4
    z, yh, core = tgt // 4, lax.rem(tgt // 2, 2), lax.rem(tgt, 2)
    up, down, far = lax.rem(z + 1, 4), lax.rem(z + 3, 4), lax.rem(z + 2, 4)
    place = z * 2 + yh

    def device(zz, hh, cc):
        return (src, zz * 4 + hh * 2 + cc)

    dev_up, dev_down = device(up, yh, core), device(down, yh, core)
    dev_y, dev_twin = device(z, 1 - yh, core), device(z, yh, 1 - core)
    peers = [lax.rem(src + d, 8) for d in range(8)]

    def at128(value):
        return pl.multiple_of(value, 128)

    def half_of(cc):
        return pl.ds(at128(cc * 1024), 1024)

    def block_of(q):
        return pl.ds(at128(core * 1024 + q * 128), 128)

    def pair_of(zz):
        return pl.ds(at128(core * 1024 + zz * 256), 256)

    def pair(zz):
        return pl.ds(at128(zz * 256), 256)

    incoming = {}

    def fetch(name, source, target, sem):
        copy = pltpu.make_async_copy(source, target, sem)
        copy.start()
        incoming[name] = copy

    for s in range(LAYERS):
        fetch(("encw", s), encw_hbm.at[s], encw_v.at[s], encw_sem.at[s])
        fetch(("res", s), res_hbm.at[s], res_v.at[s], res_sem.at[s])
        fetch(("act", s), act_hbm.at[s], act_v.at[s], act_sem.at[s])
    for j in range(16):
        cc, q = j % 2, j // 2
        fetch(
            ("w", j),
            decw_hbm.at[:, :, pl.ds(j * 128, 128)],
            w_v.at[:, :, pl.ds(cc * 1024 + q * 128, 128)],
            w_sem.at[j],
        )
    fetch("tgt", tgt_hbm.at[x], tgt_v, tgt_sem)

    for s in range(LAYERS):
        for t in range(s, LAYERS):
            found = jnp.int32(0)
            for k in range(10):
                hit = jnp.logical_and(pairs_ref[k, 0] == s, pairs_ref[k, 1] == t)
                found = jnp.where(hit, jnp.int32(k), found)
            row_s[s * 4 + t] = found

    barrier = pltpu.get_barrier_semaphore()
    greeted = [dev_up, dev_down, dev_y, dev_twin] + [(peers[d], tgt) for d in range(1, 8)]
    for other in greeted:
        pl.semaphore_signal(barrier, inc=1, device_id=other, device_id_type=MESH)
    pl.semaphore_wait(barrier, len(greeted))

    sent = []

    def remote(source, target, send_sem, recv_sem, dev):
        return pltpu.make_async_remote_copy(
            src_ref=source, dst_ref=target, send_sem=send_sem, recv_sem=recv_sem,
            device_id=dev, device_id_type=MESH,
        )

    def gather_copy(i, kind):
        lat = lat_v.at[i]
        if kind in (A_Y, A_OWN_UP, A_OWN_DOWN):
            view = lat.at[:, block_of(place)]
        elif kind in (A_PAIR_UP, A_PAIR_DOWN):
            view = lat.at[:, block_of(z * 2 + 1 - yh)]
        elif kind == A_FWD_UP:
            view = lat.at[pl.ds(0, part), pair_of(down)]
        elif kind == A_FWD_DOWN:
            view = lat.at[pl.ds(part, part), pair_of(up)]
        else:
            view = lat.at[:, half_of(core)]
        if kind == A_Y:
            dev = dev_y
        elif kind == A_TWIN:
            dev = dev_twin
        elif kind in (A_OWN_UP, A_PAIR_UP, A_FWD_UP):
            dev = dev_up
        else:
            dev = dev_down
        return remote(view, view, a_send.at[i, kind], a_recv.at[i, kind], dev)

    def scatter_copy(i, kind):
        if kind == R_TWIN:
            source, target, dev = g_v.at[i, :, half_of(1 - core)], tw_v.at[i], dev_twin
        elif kind == R_RELAY_UP:
            source, target, dev = s_v.at[i, pl.ds(0, part), pair(far)], zr_v.at[i, 0], dev_up
        elif kind == R_RELAY_DOWN:
            source, target, dev = s_v.at[i, pl.ds(part, part), pair(far)], zr_v.at[i, 1], dev_down
        elif kind == R_LAST_UP:
            source, target, dev = s_v.at[i, :, pair(up)], zf_v.at[i, 0], dev_up
        elif kind == R_LAST_DOWN:
            source, target, dev = s_v.at[i, :, pair(down)], zf_v.at[i, 1], dev_down
        else:
            source, target, dev = ty_v.at[i], yr_v.at[i], dev_y
        return remote(source, target, r_send.at[i, kind], r_recv.at[i, kind], dev)

    def part_copy(h, d):
        peer = peers[d]
        source = p_snd.at[h, lax.rem(peer, 4), :, pl.ds(at128((peer // 4) * 128), 128)]
        return remote(source, p_rcv.at[h, d], p_send.at[h, d], p_recv.at[h, d], (peer, tgt))

    def error_copy(h, d):
        view = err_v.at[h, x, :, pl.ds(at128(yl * 128), 128)]
        return remote(view, view, e_send.at[h, d], e_recv.at[h, d], (peers[d], tgt))

    def start(copy):
        copy.start()
        sent.append(copy)

    def encode(h, s):
        i = h * 4 + s
        if h == 0:
            for name in ("encw", "res", "act"):
                incoming[(name, s)].wait()
        rows = pl.ds(h * chunk, chunk)
        pre = jnp.dot(res_v[s, rows, :], encw_v[s], preferred_element_type=F32)
        pre = pre + encb_ref[s : s + 1, :]
        lat_v[i, :, block_of(place)] = (pre * act_v[s, rows, :].astype(F32)).astype(BF16)
        for kind in (A_Y, A_OWN_UP, A_OWN_DOWN):
            start(gather_copy(i, kind))

    def gather_pair(i):
        gather_copy(i, A_Y).wait_recv()
        start(gather_copy(i, A_PAIR_UP))
        start(gather_copy(i, A_PAIR_DOWN))

    def gather_forward(i):
        gather_copy(i, A_OWN_UP).wait_recv()
        gather_copy(i, A_PAIR_UP).wait_recv()
        start(gather_copy(i, A_FWD_UP))
        gather_copy(i, A_OWN_DOWN).wait_recv()
        gather_copy(i, A_PAIR_DOWN).wait_recv()
        start(gather_copy(i, A_FWD_DOWN))

    def gather_twin(i):
        gather_copy(i, A_FWD_UP).wait_recv()
        gather_copy(i, A_FWD_DOWN).wait_recv()
        start(gather_copy(i, A_TWIN))

    def recon(h, s):
        i = h * 4 + s
        gather_copy(i, A_TWIN).wait_recv()
        if i == 0:
            for j in range(16):
                incoming[("w", j)].wait()
        for t in range(s, LAYERS):
            term = lax.dot_general(
                w_v[row_s[s * 4 + t]], lat_v[i], (((1,), (1,)), ((), ())),
                preferred_element_type=F32,
            )
            if s == 0:
                p_acc[h, t] = term
            else:
                p_acc[h, t] = p_acc[h, t] + term

    def share_parts(h):
        p_snd[h] = p_acc[h].astype(BF16)
        for d in range(1, 8):
            start(part_copy(h, d))

    def make_error(h):
        own = pl.ds(at128(yl * 128), 128)
        total = p_acc[h, x, :, own]
        for d in range(1, 8):
            part_copy(h, d).wait_recv()
            total = total + p_rcv[h, d].astype(F32)
        if h == 0:
            incoming["tgt"].wait()
        bias = column_of(decb_ref[pl.ds(x, 1), :], feats)
        wanted = tgt_v[:, pl.ds(at128(h * chunk + yl * 128), 128)].astype(F32)
        err_v[h, x, :, own] = (total + bias - wanted).astype(BF16)
        for d in range(1, 8):
            start(error_copy(h, d))

    def have_error(h):
        for d in range(1, 8):
            error_copy(h, d).wait_recv()

    def grad(h, s):
        i = h * 4 + s
        count = LAYERS - s
        err = err_v[h, s:].reshape(count * feats, chunk)
        step = 512

        @pl.loop(0, 2048 // step)
        def _(n):
            cols = pl.ds(pl.multiple_of(n * step, step), step)
            weights = [w_v[row_s[s * 4 + t], :, cols] for t in range(s, LAYERS)]
            stack = jnp.concatenate(weights, axis=0) if count > 1 else weights[0]
            g_v[i, :, cols] = lax.dot_general(
                err, stack, (((0,), (0,)), ((), ())), preferred_element_type=F32
            ).astype(BF16)

        start(scatter_copy(i, R_TWIN))

    def scatter_twin(i):
        scatter_copy(i, R_TWIN).wait_recv()
        s_v[i] = (g_v[i, :, half_of(core)].astype(F32) + tw_v[i].astype(F32)).astype(BF16)
        start(scatter_copy(i, R_RELAY_UP))
        start(scatter_copy(i, R_RELAY_DOWN))

    def scatter_relay(i):
        for kind, rows, to, slot, last in (
            (R_RELAY_UP, pl.ds(0, part), up, 0, R_LAST_UP),
            (R_RELAY_DOWN, pl.ds(part, part), down, 1, R_LAST_DOWN),
        ):
            scatter_copy(i, kind).wait_recv()
            mine = s_v[i, rows, pair(to)].astype(F32)
            s_v[i, rows, pair(to)] = (mine + zr_v[i, slot].astype(F32)).astype(BF16)
            start(scatter_copy(i, last))

    def column_sum(i, hh):
        inner = pl.ds(at128(hh * 128), 128)
        mine = s_v[i, :, pl.ds(at128(z * 256 + hh * 128), 128)].astype(F32)
        return mine + zf_v[i, 0, :, inner].astype(F32) + zf_v[i, 1, :, inner].astype(F32)

    def scatter_last(i):
        scatter_copy(i, R_LAST_UP).wait_recv()
        scatter_copy(i, R_LAST_DOWN).wait_recv()
        ty_v[i] = column_sum(i, 1 - yh).astype(BF16)
        start(scatter_copy(i, R_Y))

    def scatter_own(h, s):
        i = h * 4 + s
        scatter_copy(i, R_Y).wait_recv()
        rows = pl.ds(h * chunk, chunk)
        grads = column_sum(i, yh) + yr_v[i].astype(F32)
        pre = (grads * act_v[s, rows, :].astype(F32)).astype(BF16)
        pre_v[s, rows, :] = pre
        sums = jnp.sum(pre.astype(F32), axis=0, keepdims=True)
        if h == 0:
            bias_ref[s : s + 1, :] = sums
        else:
            bias_ref[s : s + 1, :] = bias_ref[s : s + 1, :] + sums

    leaving = {}

    def encoder_grad(s, slot):
        if ("enc", slot) in leaving:
            leaving.pop(("enc", slot)).wait()

        @pl.loop(0, width // 256)
        def _(n):
            cols = pl.ds(pl.multiple_of(n * 256, 256), 256)
            eo_v[slot, cols, :] = lax.dot_general(
                res_v[s, :, cols], pre_v[s], (((0,), (0,)), ((), ())), preferred_element_type=F32
            ).astype(BF16)

        copy = pltpu.make_async_copy(eo_v.at[slot], enc_hbm.at[s], eo_sem.at[slot])
        copy.start()
        leaving[("enc", slot)] = copy

    def decoder_grad(k):
        slot = k % 2
        if ("dec", slot) in leaving:
            leaving.pop(("dec", slot)).wait()
        source, target = pairs_ref[k, 0], pairs_ref[k, 1]
        low, high = err_v[0, target], err_v[1, target]
        for cc in range(2):
            for m in range(2):
                cols = slice(cc * 1024 + m * 512, cc * 1024 + (m + 1) * 512)
                out = jnp.dot(low, lat_v[source, :, cols], preferred_element_type=F32)
                out = out + jnp.dot(high, lat_v[source + 4, :, cols], preferred_element_type=F32)
                out = out.astype(BF16)
                for j in range(4):
                    begin = ((m * 4 + j) * 2 + cc) * 128
                    dst_v[slot, :, begin : begin + 128] = out[:, j * 128 : (j + 1) * 128]
        copy = pltpu.make_async_copy(dst_v.at[slot], dec_hbm.at[k], dst_sem.at[slot])
        copy.start()
        leaving[("dec", slot)] = copy

    for h in range(HALVES):
        for s in range(LAYERS):
            encode(h, s)
    for step in range(ITEMS + 3):
        if step < ITEMS:
            gather_pair(step)
        if 0 <= step - 1 < ITEMS:
            gather_forward(step - 1)
        if 0 <= step - 2 < ITEMS:
            gather_twin(step - 2)
        if step - 3 >= 0:
            recon((step - 3) // 4, (step - 3) % 4)
        if step == 6:
            share_parts(0)
        if step == 8:
            make_error(0)
    share_parts(1)
    have_error(0)
    order = [(h, s) for h in range(HALVES) for s in reversed(range(LAYERS))]
    index = [h * 4 + s for h, s in order]
    rows_done = 0
    for step in range(ITEMS + 4):
        if step == 4:
            have_error(1)
        if step < ITEMS:
            grad(*order[step])
        if step == 1:
            make_error(1)
        if 0 <= step - 1 < ITEMS:
            scatter_twin(index[step - 1])
        if 0 <= step - 2 < ITEMS:
            scatter_relay(index[step - 2])
        if 0 <= step - 3 < ITEMS:
            scatter_last(index[step - 3])
        if step - 4 >= 0:
            h, s = order[step - 4]
            scatter_own(h, s)
            if h == 1:
                encoder_grad(s, s % 2)
        if step >= 4:
            for _ in range(2):
                if rows_done < 10:
                    decoder_grad(rows_done)
                    rows_done += 1
    for copy in leaving.values():
        copy.wait()
    for copy in sent:
        copy.wait_send()


def shards(residual, targets, enc_weight, enc_bias, active, dec_weight, dec_bias, tile_pairs):
    layers, tok, width = residual.shape
    feats = targets.shape[1]
    own = enc_weight.shape[2]
    rows, _, block = dec_weight.shape
    chunk = tok // HALVES
    any_space = pl.BlockSpec(memory_space=pl.ANY)
    vmem = pl.BlockSpec(memory_space=pltpu.VMEM)
    dma = pltpu.SemaphoreType.DMA
    return pl.pallas_call(
        kernel,
        out_shape=(
            jax.ShapeDtypeStruct((rows, feats, block), BF16),
            jax.ShapeDtypeStruct((layers, width, own), BF16),
            jax.ShapeDtypeStruct((layers, own), F32),
        ),
        in_specs=[
            any_space, any_space, any_space, vmem, any_space, any_space, vmem,
            pl.BlockSpec(memory_space=pltpu.SMEM),
        ],
        out_specs=(any_space, any_space, vmem),
        scratch_shapes=[
            pltpu.VMEM((layers, tok, width), BF16),
            pltpu.VMEM((feats, tok), BF16),
            pltpu.VMEM((layers, width, own), BF16),
            pltpu.VMEM((layers, tok, own), jnp.int32),
            pltpu.VMEM((rows, feats, block), BF16),
            pltpu.VMEM((ITEMS, chunk, block), BF16),
            pltpu.VMEM((HALVES, layers, feats, chunk), F32),
            pltpu.VMEM((HALVES, layers, feats, chunk), BF16),
            pltpu.VMEM((HALVES, 8, feats, 128), BF16),
            pltpu.VMEM((HALVES, layers, feats, chunk), BF16),
            pltpu.VMEM((ITEMS, chunk, block), BF16),
            pltpu.VMEM((ITEMS, chunk, block // 2), BF16),
            pltpu.VMEM((ITEMS, chunk, block // 2), BF16),
            pltpu.VMEM((ITEMS, 2, chunk // 2, 256), BF16),
            pltpu.VMEM((ITEMS, 2, chunk, 256), BF16),
            pltpu.VMEM((ITEMS, chunk, own), BF16),
            pltpu.VMEM((ITEMS, chunk, own), BF16),
            pltpu.VMEM((layers, tok, own), BF16),
            pltpu.VMEM((2, feats, block), BF16),
            pltpu.VMEM((2, width, own), BF16),
            pltpu.SMEM((16,), jnp.int32),
            dma((layers,)), dma((layers,)), dma((layers,)), dma((16,)), dma, dma((2,)), dma((2,)),
            dma((ITEMS, 8)), dma((ITEMS, 8)), dma((ITEMS, 6)), dma((ITEMS, 6)),
            dma((HALVES, 8)), dma((HALVES, 8)), dma((HALVES, 8)), dma((HALVES, 8)),
        ],
        compiler_params=pltpu.CompilerParams(
            collective_id=0, has_side_effects=True, vmem_limit_bytes=67043328
        ),
    )(residual, targets, enc_weight, enc_bias, active, dec_weight, dec_bias, tile_pairs)


def solution(mesh):
    in_specs = (
        P(),
        P(None, "tgt", None),
        P(None, None, ("src", "tgt")),
        P(None, ("src", "tgt")),
        P(None, None, ("src", "tgt")),
        P("src", "tgt", None),
        P(None, "tgt"),
        P("src", None),
    )
    out_specs = (P("src", "tgt", None), P(None, None, ("src", "tgt")), P(None, ("src", "tgt")))
    return jax.shard_map(shards, mesh=mesh, in_specs=in_specs, out_specs=out_specs, check_vma=False)
```

```python
import functools

import jax
import jax.numpy as jnp
from jax import lax
from jax.experimental import pallas as pl
from jax.experimental.pallas import tpu as pltpu
from jax.sharding import PartitionSpec as P

MESH = pl.DeviceIdType.MESH
F32 = jnp.float32
BF16 = jnp.bfloat16
LAYERS = 4
HALVES = 2
ITEMS = LAYERS * HALVES
A_Y, A_OWN_UP, A_OWN_DOWN, A_PAIR_UP, A_PAIR_DOWN, A_FWD_UP, A_FWD_DOWN, A_FAR, A_TWIN = range(9)
R_TWIN, R_FAR, R_SIDE_UP, R_SIDE_DOWN, R_RELAY_UP, R_RELAY_DOWN, R_OWN_UP, R_OWN_DOWN, R_Y = range(9)


def column_of(row, size):
    down = lax.broadcasted_iota(jnp.int32, (size, size), 0)
    across = lax.broadcasted_iota(jnp.int32, (size, size), 1)
    spread = jnp.where(down == across, jnp.broadcast_to(row, (size, size)), 0.0)
    return jnp.sum(spread, axis=1, keepdims=True)


def kernel(
    res_hbm, tgt_hbm, encw_hbm, encb_ref, act_hbm, decw_hbm, decb_ref, pairs_ref,
    dec_ref, enc_ref, bias_ref,
    res_v, tgt_v, encw_v, act_v, w_v, lat_v, p_acc, p_snd, p_rcv, err_v, g_v, tw_v, s_v,
    fy_v, zr_v, zf_v, ty_v, yr_v, pre_v, et_v, row_s,
    res_sem, encw_sem, act_sem, w_sem, tgt_sem,
    a_send, a_recv, r_send, r_recv, p_send, p_recv, e_send, e_recv,
):
    tok = tgt_v.shape[1]
    chunk = tok // HALVES
    part = chunk // 2
    feats = w_v.shape[1]
    blocks = res_v.shape[1]

    src = lax.axis_index("src")
    tgt = lax.axis_index("tgt")
    x, yl = lax.rem(src, 4), src // 4
    z, yh, core = tgt // 4, lax.rem(tgt // 2, 2), lax.rem(tgt, 2)
    up, down, far = lax.rem(z + 1, 4), lax.rem(z + 3, 4), lax.rem(z + 2, 4)
    place = z * 2 + yh

    def device(zz, hh, cc):
        return (src, zz * 4 + hh * 2 + cc)

    dev_up, dev_down = device(up, yh, core), device(down, yh, core)
    dev_y, dev_twin = device(z, 1 - yh, core), device(z, yh, 1 - core)
    peers = [lax.rem(src + d, 8) for d in range(8)]

    def at128(value):
        return pl.multiple_of(value, 128)

    def half_of(cc):
        return pl.ds(at128(cc * 1024), 1024)

    def block_of(q):
        return pl.ds(at128(core * 1024 + q * 128), 128)

    barrier = pltpu.get_barrier_semaphore()
    greeted = [dev_up, dev_down, dev_y, dev_twin] + [(peers[d], tgt) for d in range(1, 8)]
    for other in greeted:
        pl.semaphore_signal(barrier, inc=1, device_id=other, device_id_type=MESH)

    incoming = {}

    def fetch(name, source, target, sem):
        copy = pltpu.make_async_copy(source, target, sem)
        copy.start()
        incoming[name] = copy

    def fetch_layer(s):
        fetch(("encw", s), encw_hbm.at[s], encw_v.at[s], encw_sem.at[s])
        fetch_tokens(0, s)
        fetch(("act", s), act_hbm.at[s], act_v.at[s], act_sem.at[s])

    def fetch_tokens(h, s):
        for n in range(blocks):
            pltpu.make_async_copy(
                res_hbm.at[s, pl.ds(h * chunk, chunk), pl.ds(n * 256, 256)],
                res_v.at[s, n, h],
                res_sem.at[s, h],
            ).start()

    def have_tokens(h, s):
        whole = res_v.at[s, :, h]
        pltpu.make_async_copy(whole, whole, res_sem.at[s, h]).wait()

    def fetch_rest():
        for j in range(16):
            cc, q = j % 2, j // 2
            fetch(
                ("w", j),
                decw_hbm.at[:, :, pl.ds(j * 128, 128)],
                w_v.at[:, :, pl.ds(cc * 1024 + q * 128, 128)],
                w_sem.at[j],
            )
        fetch("tgt", tgt_hbm.at[x], tgt_v, tgt_sem)

    fetch_layer(0)
    fetch_layer(1)

    for s in range(LAYERS):
        for t in range(s, LAYERS):
            found = jnp.int32(0)
            for k in range(10):
                hit = jnp.logical_and(pairs_ref[0, k] == s, pairs_ref[1, k] == t)
                found = jnp.where(hit, jnp.int32(k), found)
            row_s[s * 4 + t] = found

    sent = []

    def remote(source, target, send_sem, recv_sem, dev):
        return pltpu.make_async_remote_copy(
            src_ref=source, dst_ref=target, send_sem=send_sem, recv_sem=recv_sem,
            device_id=dev, device_id_type=MESH,
        )

    def gather_copy(i, kind):
        lat = lat_v.at[i]
        if kind in (A_Y, A_OWN_UP, A_OWN_DOWN):
            view = lat.at[:, block_of(place)]
        elif kind in (A_PAIR_UP, A_PAIR_DOWN):
            view = lat.at[:, block_of(z * 2 + 1 - yh)]
        elif kind == A_FWD_UP:
            view = lat.at[pl.ds(0, part), block_of(down * 2 + yh)]
        elif kind == A_FWD_DOWN:
            view = lat.at[pl.ds(part, part), block_of(up * 2 + yh)]
        elif kind == A_FAR:
            view = lat.at[:, block_of(far * 2 + yh)]
        else:
            view = lat.at[:, half_of(core)]
        if kind in (A_Y, A_FAR):
            dev = dev_y
        elif kind == A_TWIN:
            dev = dev_twin
        elif kind in (A_OWN_UP, A_PAIR_UP, A_FWD_UP):
            dev = dev_up
        else:
            dev = dev_down
        return remote(view, view, a_send.at[i, kind], a_recv.at[i, kind], dev)

    def spot(zz, hh):
        return pl.ds(at128(zz * 256 + hh * 128), 128)

    def scatter_copy(i, kind):
        other = 1 - yh
        if kind == R_TWIN:
            source, target, dev = g_v.at[i, :, half_of(1 - core)], tw_v.at[i], dev_twin
        elif kind == R_FAR:
            source, target, dev = s_v.at[i, :, spot(far, other)], fy_v.at[i], dev_y
        elif kind == R_SIDE_UP:
            source, target, dev = s_v.at[i, :, spot(up, other)], zf_v.at[i, 0, 1], dev_up
        elif kind == R_SIDE_DOWN:
            source, target, dev = s_v.at[i, :, spot(down, other)], zf_v.at[i, 1, 1], dev_down
        elif kind == R_RELAY_UP:
            source, target, dev = s_v.at[i, pl.ds(0, part), spot(far, yh)], zr_v.at[i, 0], dev_up
        elif kind == R_RELAY_DOWN:
            source, target, dev = s_v.at[i, pl.ds(part, part), spot(far, yh)], zr_v.at[i, 1], dev_down
        elif kind == R_OWN_UP:
            source, target, dev = s_v.at[i, :, spot(up, yh)], zf_v.at[i, 0, 0], dev_up
        elif kind == R_OWN_DOWN:
            source, target, dev = s_v.at[i, :, spot(down, yh)], zf_v.at[i, 1, 0], dev_down
        else:
            source, target, dev = ty_v.at[i], yr_v.at[i], dev_y
        return remote(source, target, r_send.at[i, kind], r_recv.at[i, kind], dev)

    def part_copy(h, d):
        peer = peers[d]
        source = p_snd.at[h, lax.rem(peer, 4), :, pl.ds(at128((peer // 4) * 128), 128)]
        return remote(source, p_rcv.at[h, d], p_send.at[h, d], p_recv.at[h, d], (peer, tgt))

    def error_copy(h, d):
        view = err_v.at[h, x, :, pl.ds(at128(yl * 128), 128)]
        return remote(view, view, e_send.at[h, d], e_recv.at[h, d], (peers[d], tgt))

    def start(copy):
        copy.start()
        sent.append(copy)

    def encode(h, s):
        i = h * 4 + s
        if h == 0:
            incoming[("encw", s)].wait()
            incoming[("act", s)].wait()
        have_tokens(h, s)
        if h == 0:
            if s < 2:
                fetch_layer(s + 2)
            else:
                fetch_tokens(1, 2 * (s - 2))
                fetch_tokens(1, 2 * (s - 2) + 1)
            if s == 3:
                fetch_rest()
        rows = pl.ds(h * chunk, chunk)
        pre = jnp.zeros((chunk, 128), F32)
        for n in range(blocks):
            weight = encw_v[s, n * 256 : (n + 1) * 256, :]
            pre = pre + jnp.dot(res_v[s, n, h], weight, preferred_element_type=F32)
        pre = pre + encb_ref[s : s + 1, :]
        lat_v[i, :, block_of(place)] = (pre * act_v[s, rows, :].astype(F32)).astype(BF16)
        if i == 0:
            pl.semaphore_wait(barrier, len(greeted))
        for kind in (A_OWN_UP, A_OWN_DOWN, A_Y):
            start(gather_copy(i, kind))

    def gather_pair(i):
        gather_copy(i, A_Y).wait_recv()
        start(gather_copy(i, A_PAIR_UP))
        start(gather_copy(i, A_PAIR_DOWN))

    def gather_forward(i):
        gather_copy(i, A_OWN_UP).wait_recv()
        start(gather_copy(i, A_FWD_UP))
        gather_copy(i, A_OWN_DOWN).wait_recv()
        start(gather_copy(i, A_FWD_DOWN))

    def gather_far(i):
        gather_copy(i, A_FWD_UP).wait_recv()
        gather_copy(i, A_FWD_DOWN).wait_recv()
        start(gather_copy(i, A_FAR))

    def gather_twin(i):
        gather_copy(i, A_PAIR_UP).wait_recv()
        gather_copy(i, A_PAIR_DOWN).wait_recv()
        gather_copy(i, A_FAR).wait_recv()
        start(gather_copy(i, A_TWIN))

    def recon(h, s):
        i = h * 4 + s
        gather_copy(i, A_TWIN).wait_recv()
        if i == 0:
            for j in range(16):
                incoming[("w", j)].wait()
        for t in range(s, LAYERS):
            term = lax.dot_general(
                w_v[row_s[s * 4 + t]], lat_v[i], (((1,), (1,)), ((), ())),
                preferred_element_type=F32,
            )
            if s == 0:
                p_acc[h, t] = term
            else:
                p_acc[h, t] = p_acc[h, t] + term

    def share_parts(h):
        p_snd[h] = p_acc[h].astype(BF16)
        for d in range(1, 8):
            start(part_copy(h, d))

    def make_error(h):
        own = pl.ds(at128(yl * 128), 128)
        total = p_acc[h, x, :, own]
        for d in range(1, 8):
            part_copy(h, d).wait_recv()
            total = total + p_rcv[h, d].astype(F32)
        if h == 0:
            incoming["tgt"].wait()
        bias = column_of(decb_ref[pl.ds(x, 1), :], feats)
        wanted = tgt_v[:, pl.ds(at128(h * chunk + yl * 128), 128)].astype(F32)
        err_v[h, x, :, own] = (total + bias - wanted).astype(BF16)
        for d in range(1, 8):
            start(error_copy(h, d))

    def have_error(h):
        for d in range(1, 8):
            error_copy(h, d).wait_recv()
        turn_error(h)

    def turn_error(h):
        stack = jnp.concatenate([err_v[h, t] for t in reversed(range(LAYERS))], axis=0)
        et_v[h] = stack.T

    def grad(h, s):
        i = h * 4 + s
        depth = (LAYERS - s) * feats
        step = 512

        @pl.loop(0, 2048 // step)
        def _(n):
            cols = pl.ds(pl.multiple_of(n * step, step), step)
            weights = [w_v[row_s[s * 4 + t], :, cols] for t in reversed(range(s, LAYERS))]
            stack = jnp.concatenate(weights, axis=0) if s < LAYERS - 1 else weights[0]
            g_v[i, :, cols] = jnp.dot(
                et_v[h, :, 0:depth], stack, preferred_element_type=F32
            ).astype(BF16)

        start(scatter_copy(i, R_TWIN))

    def scatter_twin(i):
        scatter_copy(i, R_TWIN).wait_recv()
        s_v[i] = (g_v[i, :, half_of(core)].astype(F32) + tw_v[i].astype(F32)).astype(BF16)
        for kind in (R_FAR, R_SIDE_UP, R_SIDE_DOWN):
            start(scatter_copy(i, kind))

    def scatter_far(i):
        scatter_copy(i, R_FAR).wait_recv()
        mine = s_v[i, :, spot(far, yh)].astype(F32)
        s_v[i, :, spot(far, yh)] = (mine + fy_v[i].astype(F32)).astype(BF16)
        start(scatter_copy(i, R_RELAY_UP))
        start(scatter_copy(i, R_RELAY_DOWN))

    def scatter_relay(i):
        for kind, rows, to, slot, last in (
            (R_RELAY_UP, pl.ds(0, part), up, 0, R_OWN_UP),
            (R_RELAY_DOWN, pl.ds(part, part), down, 1, R_OWN_DOWN),
        ):
            scatter_copy(i, kind).wait_recv()
            mine = s_v[i, rows, spot(to, yh)].astype(F32)
            s_v[i, rows, spot(to, yh)] = (mine + zr_v[i, slot].astype(F32)).astype(BF16)
            start(scatter_copy(i, last))

    def scatter_side(i):
        scatter_copy(i, R_SIDE_UP).wait_recv()
        scatter_copy(i, R_SIDE_DOWN).wait_recv()
        total = s_v[i, :, spot(z, 1 - yh)].astype(F32)
        ty_v[i] = (total + zf_v[i, 0, 1].astype(F32) + zf_v[i, 1, 1].astype(F32)).astype(BF16)
        start(scatter_copy(i, R_Y))

    def scatter_own(h, s):
        i = h * 4 + s
        scatter_copy(i, R_Y).wait_recv()
        grads = s_v[i, :, spot(z, yh)].astype(F32) + yr_v[i].astype(F32)
        scatter_copy(i, R_OWN_UP).wait_recv()
        scatter_copy(i, R_OWN_DOWN).wait_recv()
        grads = grads + zf_v[i, 0, 0].astype(F32) + zf_v[i, 1, 0].astype(F32)
        rows = pl.ds(h * chunk, chunk)
        pre = (grads * act_v[s, rows, :].astype(F32)).astype(BF16)
        pre_v[s, rows, :] = pre
        sums = jnp.sum(pre.astype(F32), axis=0, keepdims=True)
        if h == 0:
            bias_ref[s : s + 1, :] = sums
        else:
            bias_ref[s : s + 1, :] = bias_ref[s : s + 1, :] + sums

    def encoder_grad(s):
        across = pre_v[s].T

        @pl.loop(0, blocks)
        def _(n):
            block = res_v[s, n].reshape(tok, 256)
            out = jnp.dot(across, block, preferred_element_type=F32).astype(BF16)
            enc_ref[s, pl.ds(pl.multiple_of(n * 256, 256), 256), :] = out.T

    def decoder_grad(k):
        source, target = pairs_ref[0, k], pairs_ref[1, k]
        low, high = err_v[0, target], err_v[1, target]
        for cc in range(2):
            for m in range(2):
                cols = slice(cc * 1024 + m * 512, cc * 1024 + (m + 1) * 512)
                out = jnp.dot(low, lat_v[source, :, cols], preferred_element_type=F32)
                out = out + jnp.dot(high, lat_v[source + 4, :, cols], preferred_element_type=F32)
                out = out.astype(BF16)
                for j in range(4):
                    begin = ((m * 4 + j) * 2 + cc) * 128
                    dec_ref[k, :, begin : begin + 128] = out[:, j * 128 : (j + 1) * 128]

    for s in range(LAYERS):
        encode(0, s)
    gather_forward(0)
    gather_forward(1)
    gather_pair(0)
    gather_forward(2)
    gather_pair(1)
    gather_forward(3)
    gather_pair(2)
    gather_pair(3)
    for s in range(LAYERS):
        encode(1, s)
        gather_far(s)
    gather_twin(0)
    gather_forward(4)
    gather_twin(1)
    gather_forward(5)
    gather_twin(2)
    recon(0, 0)
    gather_forward(6)
    gather_pair(4)
    gather_twin(3)
    recon(0, 1)
    gather_forward(7)
    gather_pair(5)
    recon(0, 2)
    gather_pair(6)
    gather_pair(7)
    recon(0, 3)
    share_parts(0)
    gather_far(4)
    gather_far(5)
    gather_far(6)
    gather_twin(4)
    make_error(0)
    gather_far(7)
    gather_twin(5)
    recon(1, 0)
    gather_twin(6)
    recon(1, 1)
    have_error(0)
    grad(0, 3)
    gather_twin(7)
    grad(0, 2)
    recon(1, 2)
    scatter_twin(3)
    recon(1, 3)
    share_parts(1)
    scatter_twin(2)
    grad(0, 1)
    scatter_far(3)
    grad(0, 0)
    scatter_twin(1)
    scatter_side(3)
    make_error(1)
    scatter_far(2)
    scatter_twin(0)
    scatter_side(2)
    scatter_relay(3)
    scatter_far(1)
    scatter_side(1)
    scatter_relay(2)
    have_error(1)
    grad(1, 3)
    grad(1, 2)
    scatter_twin(7)
    scatter_own(0, 3)
    scatter_far(0)
    scatter_side(0)
    scatter_relay(1)
    grad(1, 1)
    scatter_twin(6)
    scatter_own(0, 2)
    scatter_relay(0)
    scatter_far(7)
    grad(1, 0)
    scatter_twin(5)
    scatter_side(7)
    scatter_own(0, 1)
    scatter_own(0, 0)
    scatter_far(6)
    scatter_twin(4)
    scatter_side(6)
    decoder_grad(0)
    decoder_grad(1)
    scatter_relay(7)
    scatter_far(5)
    scatter_side(5)
    decoder_grad(2)
    decoder_grad(3)
    scatter_relay(6)
    scatter_far(4)
    scatter_side(4)
    decoder_grad(4)
    decoder_grad(5)
    scatter_own(1, 3)
    scatter_relay(5)
    encoder_grad(3)
    decoder_grad(6)
    scatter_relay(4)
    scatter_own(1, 2)
    encoder_grad(2)
    decoder_grad(7)
    decoder_grad(8)
    scatter_own(1, 1)
    encoder_grad(1)
    decoder_grad(9)
    scatter_own(1, 0)
    encoder_grad(0)
    for copy in sent:
        copy.wait_send()


def deliver(dec_ref, enc_ref, bias_ref, dec_out, enc_out, bias_out, sem):
    copies = [
        pltpu.make_async_copy(one, out, sem.at[n])
        for n, (one, out) in enumerate(((dec_ref, dec_out), (enc_ref, enc_out), (bias_ref, bias_out)))
    ]
    for copy in copies:
        copy.start()
    for copy in copies:
        copy.wait()


def shards(residual, targets, enc_weight, enc_bias, active, dec_weight, dec_bias, tile_pairs):
    layers, tok, width = residual.shape
    feats = targets.shape[1]
    own = enc_weight.shape[2]
    rows, _, block = dec_weight.shape
    chunk = tok // HALVES
    any_space = pl.BlockSpec(memory_space=pl.ANY)
    vmem = pl.BlockSpec(memory_space=pltpu.VMEM)
    dma = pltpu.SemaphoreType.DMA
    blocks = width // 256
    held = pl.pallas_call(
        kernel,
        out_shape=(
            pltpu.VMEM((rows, feats, block), BF16),
            pltpu.VMEM((layers, width, own), BF16),
            pltpu.VMEM((layers, own), F32),
        ),
        in_specs=[
            any_space, any_space, any_space, vmem, any_space, any_space, vmem,
            pl.BlockSpec(memory_space=pltpu.SMEM),
        ],
        out_specs=(vmem, vmem, vmem),
        scratch_shapes=[
            pltpu.VMEM((layers, blocks, HALVES, chunk, 256), BF16),
            pltpu.VMEM((feats, tok), BF16),
            pltpu.VMEM((layers, width, own), BF16),
            pltpu.VMEM((layers, tok, own), jnp.int32),
            pltpu.VMEM((rows, feats, block), BF16),
            pltpu.VMEM((ITEMS, chunk, block), BF16),
            pltpu.VMEM((HALVES, layers, feats, chunk), F32),
            pltpu.VMEM((HALVES, layers, feats, chunk), BF16),
            pltpu.VMEM((HALVES, 8, feats, 128), BF16),
            pltpu.VMEM((HALVES, layers, feats, chunk), BF16),
            pltpu.VMEM((ITEMS, chunk, block), BF16),
            pltpu.VMEM((ITEMS, chunk, block // 2), BF16),
            pltpu.VMEM((ITEMS, chunk, block // 2), BF16),
            pltpu.VMEM((ITEMS, chunk, own), BF16),
            pltpu.VMEM((ITEMS, 2, chunk // 2, own), BF16),
            pltpu.VMEM((ITEMS, 2, 2, chunk, own), BF16),
            pltpu.VMEM((ITEMS, chunk, own), BF16),
            pltpu.VMEM((ITEMS, chunk, own), BF16),
            pltpu.VMEM((layers, tok, own), BF16),
            pltpu.VMEM((HALVES, chunk, layers * feats), BF16),
            pltpu.SMEM((16,), jnp.int32),
            dma((layers, HALVES)), dma((layers,)), dma((layers,)), dma((16,)), dma,
            dma((ITEMS, 9)), dma((ITEMS, 9)), dma((ITEMS, 9)), dma((ITEMS, 9)),
            dma((HALVES, 8)), dma((HALVES, 8)), dma((HALVES, 8)), dma((HALVES, 8)),
        ],
        compiler_params=pltpu.CompilerParams(
            collective_id=0, has_side_effects=True, vmem_limit_bytes=58000000
        ),
    )(residual, targets, enc_weight, enc_bias, active, dec_weight, dec_bias, tile_pairs.T)
    return pl.pallas_call(
        deliver,
        out_shape=tuple(jax.ShapeDtypeStruct(one.shape, one.dtype) for one in held),
        in_specs=[any_space] * 3,
        out_specs=(any_space,) * 3,
        scratch_shapes=[dma((3,))],
        compiler_params=pltpu.CompilerParams(vmem_limit_bytes=1 << 20),
    )(*held)


def solution(mesh):
    in_specs = (
        P(),
        P(None, "tgt", None),
        P(None, None, ("src", "tgt")),
        P(None, ("src", "tgt")),
        P(None, None, ("src", "tgt")),
        P("src", "tgt", None),
        P(None, "tgt"),
        P("src", None),
    )
    out_specs = (P("src", "tgt", None), P(None, None, ("src", "tgt")), P(None, ("src", "tgt")))
    return jax.shard_map(shards, mesh=mesh, in_specs=in_specs, out_specs=out_specs, check_vma=False)
```

```python
import functools

import jax
import jax.numpy as jnp
from jax import lax
from jax.experimental import pallas as pl
from jax.experimental.pallas import tpu as pltpu
from jax.sharding import PartitionSpec as P

MESH = pl.DeviceIdType.MESH
F32 = jnp.float32
BF16 = jnp.bfloat16
LAYERS = 4
HALVES = 2
ITEMS = LAYERS * HALVES
A_Y, A_OWN_UP, A_OWN_DOWN, A_PAIR_UP, A_PAIR_DOWN, A_FWD_UP, A_FWD_DOWN, A_FAR, A_TWIN = range(9)
R_TWIN, R_FAR, R_SIDE_UP, R_SIDE_DOWN, R_RELAY_UP, R_RELAY_DOWN, R_OWN_UP, R_OWN_DOWN, R_Y = range(9)


def column_of(row, size):
    down = lax.broadcasted_iota(jnp.int32, (size, size), 0)
    across = lax.broadcasted_iota(jnp.int32, (size, size), 1)
    spread = jnp.where(down == across, jnp.broadcast_to(row, (size, size)), 0.0)
    return jnp.sum(spread, axis=1, keepdims=True)


def kernel(
    res_hbm, tgt_hbm, encw_hbm, encb_ref, act_hbm, decw_hbm, decb_ref, pairs_ref,
    dec_ref, enc_ref, bias_ref,
    res_v, tgt_v, encw_v, act_v, w_v, lat_v, p_acc, p_snd, p_rcv, err_v, g_v, tw_v, s_v,
    fy_v, zr_v, zf_v, ty_v, yr_v, pre_v, et_v, row_s,
    res_sem, encw_sem, act_sem, w_sem, tgt_sem,
    a_send, a_recv, r_send, r_recv, p_send, p_recv, e_send, e_recv,
):
    tok = tgt_v.shape[1]
    chunk = tok // HALVES
    part = chunk // 2
    feats = w_v.shape[1]
    blocks = res_v.shape[1]

    src = lax.axis_index("src")
    tgt = lax.axis_index("tgt")
    x, yl = lax.rem(src, 4), src // 4
    z, yh, core = tgt // 4, lax.rem(tgt // 2, 2), lax.rem(tgt, 2)
    up, down, far = lax.rem(z + 1, 4), lax.rem(z + 3, 4), lax.rem(z + 2, 4)
    place = z * 2 + yh

    def device(zz, hh, cc):
        return (src, zz * 4 + hh * 2 + cc)

    dev_up, dev_down = device(up, yh, core), device(down, yh, core)
    dev_y, dev_twin = device(z, 1 - yh, core), device(z, yh, 1 - core)
    peers = [lax.rem(src + d, 8) for d in range(8)]

    def at128(value):
        return pl.multiple_of(value, 128)

    def half_of(cc):
        return pl.ds(at128(cc * 1024), 1024)

    def block_of(q):
        return pl.ds(at128(core * 1024 + q * 128), 128)

    barrier = pltpu.get_barrier_semaphore()
    greeted = [dev_up, dev_down, dev_y, dev_twin] + [(peers[d], tgt) for d in range(1, 8)]
    for other in greeted:
        pl.semaphore_signal(barrier, inc=1, device_id=other, device_id_type=MESH)

    incoming = {}

    def fetch(name, source, target, sem):
        copy = pltpu.make_async_copy(source, target, sem)
        copy.start()
        incoming[name] = copy

    def fetch_layer(s):
        fetch(("encw", s), encw_hbm.at[s], encw_v.at[s], encw_sem.at[s])
        fetch_tokens(0, s)
        fetch(("act", s), act_hbm.at[s], act_v.at[s], act_sem.at[s])

    def fetch_tokens(h, s):
        for n in range(blocks):
            pltpu.make_async_copy(
                res_hbm.at[s, pl.ds(h * chunk, chunk), pl.ds(n * 256, 256)],
                res_v.at[s, n, h],
                res_sem.at[s, h],
            ).start()

    def have_tokens(h, s):
        whole = res_v.at[s, :, h]
        pltpu.make_async_copy(whole, whole, res_sem.at[s, h]).wait()

    def fetch_rest():
        for j in range(16):
            cc, q = j % 2, j // 2
            fetch(
                ("w", j),
                decw_hbm.at[:, :, pl.ds(j * 128, 128)],
                w_v.at[:, :, pl.ds(cc * 1024 + q * 128, 128)],
                w_sem.at[j],
            )
        fetch("tgt", tgt_hbm.at[x], tgt_v, tgt_sem)

    fetch_layer(0)
    fetch_layer(1)

    for s in range(LAYERS):
        for t in range(s, LAYERS):
            found = jnp.int32(0)
            for k in range(10):
                hit = jnp.logical_and(pairs_ref[0, k] == s, pairs_ref[1, k] == t)
                found = jnp.where(hit, jnp.int32(k), found)
            row_s[s * 4 + t] = found

    sent = []

    def remote(source, target, send_sem, recv_sem, dev):
        return pltpu.make_async_remote_copy(
            src_ref=source, dst_ref=target, send_sem=send_sem, recv_sem=recv_sem,
            device_id=dev, device_id_type=MESH,
        )

    def gather_copy(i, kind):
        lat = lat_v.at[i]
        if kind in (A_Y, A_OWN_UP, A_OWN_DOWN):
            view = lat.at[:, block_of(place)]
        elif kind in (A_PAIR_UP, A_PAIR_DOWN):
            view = lat.at[:, block_of(z * 2 + 1 - yh)]
        elif kind == A_FWD_UP:
            view = lat.at[pl.ds(0, part), block_of(down * 2 + yh)]
        elif kind == A_FWD_DOWN:
            view = lat.at[pl.ds(part, part), block_of(up * 2 + yh)]
        elif kind == A_FAR:
            view = lat.at[:, block_of(far * 2 + yh)]
        else:
            view = lat.at[:, half_of(core)]
        if kind in (A_Y, A_FAR):
            dev = dev_y
        elif kind == A_TWIN:
            dev = dev_twin
        elif kind in (A_OWN_UP, A_PAIR_UP, A_FWD_UP):
            dev = dev_up
        else:
            dev = dev_down
        return remote(view, view, a_send.at[i, kind], a_recv.at[i, kind], dev)

    def spot(zz, hh):
        return pl.ds(at128(zz * 256 + hh * 128), 128)

    def scatter_copy(i, kind):
        other = 1 - yh
        if kind == R_TWIN:
            source, target, dev = g_v.at[i, :, half_of(1 - core)], tw_v.at[i], dev_twin
        elif kind == R_FAR:
            source, target, dev = s_v.at[i, :, spot(far, other)], fy_v.at[i], dev_y
        elif kind == R_SIDE_UP:
            source, target, dev = s_v.at[i, :, spot(up, other)], zf_v.at[i, 0, 1], dev_up
        elif kind == R_SIDE_DOWN:
            source, target, dev = s_v.at[i, :, spot(down, other)], zf_v.at[i, 1, 1], dev_down
        elif kind == R_RELAY_UP:
            source, target, dev = s_v.at[i, pl.ds(0, part), spot(far, yh)], zr_v.at[i, 0], dev_up
        elif kind == R_RELAY_DOWN:
            source, target, dev = s_v.at[i, pl.ds(part, part), spot(far, yh)], zr_v.at[i, 1], dev_down
        elif kind == R_OWN_UP:
            source, target, dev = s_v.at[i, :, spot(up, yh)], zf_v.at[i, 0, 0], dev_up
        elif kind == R_OWN_DOWN:
            source, target, dev = s_v.at[i, :, spot(down, yh)], zf_v.at[i, 1, 0], dev_down
        else:
            source, target, dev = ty_v.at[i], yr_v.at[i], dev_y
        return remote(source, target, r_send.at[i, kind], r_recv.at[i, kind], dev)

    def part_copy(h, d):
        peer = peers[d]
        source = p_snd.at[h, lax.rem(peer, 4), :, pl.ds(at128((peer // 4) * 128), 128)]
        return remote(source, p_rcv.at[h, d], p_send.at[h, d], p_recv.at[h, d], (peer, tgt))

    def error_copy(h, d):
        view = err_v.at[h, x, :, pl.ds(at128(yl * 128), 128)]
        return remote(view, view, e_send.at[h, d], e_recv.at[h, d], (peers[d], tgt))

    def start(copy):
        copy.start()
        sent.append(copy)

    def encode(h, s):
        i = h * 4 + s
        if h == 0:
            incoming[("encw", s)].wait()
            incoming[("act", s)].wait()
        have_tokens(h, s)
        if h == 0:
            if s < 2:
                fetch_layer(s + 2)
            else:
                fetch_tokens(1, 2 * (s - 2))
                fetch_tokens(1, 2 * (s - 2) + 1)
            if s == 3:
                fetch_rest()
        rows = pl.ds(h * chunk, chunk)
        pre = jnp.zeros((chunk, 128), F32)
        for n in range(blocks):
            weight = encw_v[s, n * 256 : (n + 1) * 256, :]
            pre = pre + jnp.dot(res_v[s, n, h], weight, preferred_element_type=F32)
        pre = pre + encb_ref[s : s + 1, :]
        lat_v[i, :, block_of(place)] = (pre * act_v[s, rows, :].astype(F32)).astype(BF16)
        if i == 0:
            pl.semaphore_wait(barrier, len(greeted))
        start(gather_copy(i, A_Y))
        if h == 0:
            send_own(i)

    def send_own(i):
        start(gather_copy(i, A_OWN_UP))
        start(gather_copy(i, A_OWN_DOWN))

    def gather_pair(i):
        gather_copy(i, A_Y).wait_recv()
        start(gather_copy(i, A_PAIR_UP))
        start(gather_copy(i, A_PAIR_DOWN))

    def gather_forward(i):
        gather_copy(i, A_OWN_UP).wait_recv()
        start(gather_copy(i, A_FWD_UP))
        gather_copy(i, A_OWN_DOWN).wait_recv()
        start(gather_copy(i, A_FWD_DOWN))

    def gather_far(i):
        gather_copy(i, A_FWD_UP).wait_recv()
        gather_copy(i, A_FWD_DOWN).wait_recv()
        start(gather_copy(i, A_FAR))

    def gather_twin(i):
        gather_copy(i, A_PAIR_UP).wait_recv()
        gather_copy(i, A_PAIR_DOWN).wait_recv()
        gather_copy(i, A_FAR).wait_recv()
        start(gather_copy(i, A_TWIN))

    def recon(h, s):
        i = h * 4 + s
        gather_copy(i, A_TWIN).wait_recv()
        if i == 0:
            for j in range(16):
                incoming[("w", j)].wait()
        for t in range(s, LAYERS):
            term = lax.dot_general(
                w_v[row_s[s * 4 + t]], lat_v[i], (((1,), (1,)), ((), ())),
                preferred_element_type=F32,
            )
            if s == 0:
                p_acc[h, t] = term
            else:
                p_acc[h, t] = p_acc[h, t] + term

    def share_parts(h):
        p_snd[h] = p_acc[h].astype(BF16)
        for d in range(1, 8):
            start(part_copy(h, d))

    def make_error(h):
        own = pl.ds(at128(yl * 128), 128)
        total = p_acc[h, x, :, own]
        for d in range(1, 8):
            part_copy(h, d).wait_recv()
            total = total + p_rcv[h, d].astype(F32)
        if h == 0:
            incoming["tgt"].wait()
        bias = column_of(decb_ref[pl.ds(x, 1), :], feats)
        wanted = tgt_v[:, pl.ds(at128(h * chunk + yl * 128), 128)].astype(F32)
        err_v[h, x, :, own] = (total + bias - wanted).astype(BF16)
        for d in range(1, 8):
            start(error_copy(h, d))

    def have_error(h):
        for d in range(1, 8):
            error_copy(h, d).wait_recv()
        turn_error(h)

    def turn_error(h):
        stack = jnp.concatenate([err_v[h, t] for t in reversed(range(LAYERS))], axis=0)
        et_v[h] = stack.T

    def grad(h, s):
        i = h * 4 + s
        depth = (LAYERS - s) * feats
        step = 512

        @pl.loop(0, 2048 // step, unroll=4)
        def _(n):
            cols = pl.ds(pl.multiple_of(n * step, step), step)
            weights = [w_v[row_s[s * 4 + t], :, cols] for t in reversed(range(s, LAYERS))]
            stack = jnp.concatenate(weights, axis=0) if s < LAYERS - 1 else weights[0]
            g_v[i, :, cols] = jnp.dot(
                et_v[h, :, 0:depth], stack, preferred_element_type=F32
            ).astype(BF16)

        start(scatter_copy(i, R_TWIN))

    def scatter_twin(i):
        scatter_copy(i, R_TWIN).wait_recv()
        s_v[i] = (g_v[i, :, half_of(core)].astype(F32) + tw_v[i].astype(F32)).astype(BF16)
        for kind in (R_FAR, R_SIDE_UP, R_SIDE_DOWN):
            start(scatter_copy(i, kind))

    def scatter_far(i):
        scatter_copy(i, R_FAR).wait_recv()
        mine = s_v[i, :, spot(far, yh)].astype(F32)
        s_v[i, :, spot(far, yh)] = (mine + fy_v[i].astype(F32)).astype(BF16)
        start(scatter_copy(i, R_RELAY_UP))
        start(scatter_copy(i, R_RELAY_DOWN))

    def scatter_relay(i):
        for kind, rows, to, slot, last in (
            (R_RELAY_UP, pl.ds(0, part), up, 0, R_OWN_UP),
            (R_RELAY_DOWN, pl.ds(part, part), down, 1, R_OWN_DOWN),
        ):
            scatter_copy(i, kind).wait_recv()
            mine = s_v[i, rows, spot(to, yh)].astype(F32)
            s_v[i, rows, spot(to, yh)] = (mine + zr_v[i, slot].astype(F32)).astype(BF16)
            start(scatter_copy(i, last))

    def scatter_side(i):
        scatter_copy(i, R_SIDE_UP).wait_recv()
        scatter_copy(i, R_SIDE_DOWN).wait_recv()
        total = s_v[i, :, spot(z, 1 - yh)].astype(F32)
        ty_v[i] = (total + zf_v[i, 0, 1].astype(F32) + zf_v[i, 1, 1].astype(F32)).astype(BF16)
        start(scatter_copy(i, R_Y))

    def scatter_own(h, s):
        i = h * 4 + s
        scatter_copy(i, R_Y).wait_recv()
        grads = s_v[i, :, spot(z, yh)].astype(F32) + yr_v[i].astype(F32)
        scatter_copy(i, R_OWN_UP).wait_recv()
        scatter_copy(i, R_OWN_DOWN).wait_recv()
        grads = grads + zf_v[i, 0, 0].astype(F32) + zf_v[i, 1, 0].astype(F32)
        rows = pl.ds(h * chunk, chunk)
        pre = (grads * act_v[s, rows, :].astype(F32)).astype(BF16)
        pre_v[s, rows, :] = pre
        sums = jnp.sum(pre.astype(F32), axis=0, keepdims=True)
        if h == 0:
            bias_ref[s : s + 1, :] = sums
        else:
            bias_ref[s : s + 1, :] = bias_ref[s : s + 1, :] + sums

    def encoder_grad(s):
        across = pre_v[s].T

        @pl.loop(0, blocks, unroll=9)
        def _(n):
            block = res_v[s, n].reshape(tok, 256)
            out = jnp.dot(across, block, preferred_element_type=F32).astype(BF16)
            enc_ref[s, pl.ds(pl.multiple_of(n * 256, 256), 256), :] = out.T

    def decoder_grad(k):
        source, target = pairs_ref[0, k], pairs_ref[1, k]
        low, high = err_v[0, target], err_v[1, target]
        for cc in range(2):
            for m in range(2):
                cols = slice(cc * 1024 + m * 512, cc * 1024 + (m + 1) * 512)
                out = jnp.dot(low, lat_v[source, :, cols], preferred_element_type=F32)
                out = out + jnp.dot(high, lat_v[source + 4, :, cols], preferred_element_type=F32)
                out = out.astype(BF16)
                for j in range(4):
                    begin = ((m * 4 + j) * 2 + cc) * 128
                    dec_ref[k, :, begin : begin + 128] = out[:, j * 128 : (j + 1) * 128]

    for s in range(LAYERS):
        encode(0, s)
    gather_forward(0)
    encode(1, 0)
    gather_forward(1)
    gather_pair(0)
    encode(1, 1)
    gather_forward(2)
    gather_pair(1)
    encode(1, 2)
    gather_forward(3)
    gather_pair(2)
    encode(1, 3)
    gather_pair(3)
    for s in range(LAYERS):
        send_own(4 + s)
    for s in range(LAYERS):
        gather_far(s)
    gather_twin(0)
    gather_forward(4)
    gather_twin(1)
    gather_forward(5)
    gather_twin(2)
    recon(0, 0)
    gather_forward(6)
    gather_pair(4)
    gather_twin(3)
    recon(0, 1)
    gather_forward(7)
    gather_pair(5)
    recon(0, 2)
    gather_pair(6)
    gather_pair(7)
    recon(0, 3)
    share_parts(0)
    gather_far(4)
    gather_far(5)
    gather_far(6)
    gather_twin(4)
    make_error(0)
    gather_far(7)
    gather_twin(5)
    recon(1, 0)
    gather_twin(6)
    recon(1, 1)
    have_error(0)
    grad(0, 3)
    gather_twin(7)
    grad(0, 2)
    recon(1, 2)
    scatter_twin(3)
    recon(1, 3)
    share_parts(1)
    scatter_twin(2)
    grad(0, 1)
    scatter_far(3)
    grad(0, 0)
    scatter_twin(1)
    scatter_side(3)
    make_error(1)
    scatter_far(2)
    scatter_twin(0)
    scatter_side(2)
    scatter_relay(3)
    scatter_far(1)
    scatter_side(1)
    scatter_relay(2)
    have_error(1)
    grad(1, 3)
    grad(1, 2)
    scatter_twin(7)
    scatter_own(0, 3)
    scatter_far(0)
    scatter_side(0)
    scatter_relay(1)
    grad(1, 1)
    scatter_twin(6)
    scatter_own(0, 2)
    scatter_relay(0)
    scatter_far(7)
    grad(1, 0)
    scatter_twin(5)
    scatter_side(7)
    scatter_own(0, 1)
    scatter_own(0, 0)
    scatter_far(6)
    scatter_twin(4)
    scatter_side(6)
    decoder_grad(0)
    decoder_grad(1)
    scatter_relay(7)
    scatter_far(5)
    scatter_side(5)
    decoder_grad(2)
    decoder_grad(3)
    scatter_relay(6)
    scatter_far(4)
    scatter_side(4)
    decoder_grad(4)
    decoder_grad(5)
    scatter_own(1, 3)
    scatter_relay(5)
    encoder_grad(3)
    decoder_grad(6)
    scatter_relay(4)
    scatter_own(1, 2)
    encoder_grad(2)
    decoder_grad(7)
    decoder_grad(8)
    scatter_own(1, 1)
    encoder_grad(1)
    decoder_grad(9)
    scatter_own(1, 0)
    encoder_grad(0)
    for copy in sent:
        copy.wait_send()


def deliver(dec_ref, enc_ref, bias_ref, dec_out, enc_out, bias_out, sem):
    copies = [
        pltpu.make_async_copy(one, out, sem.at[n])
        for n, (one, out) in enumerate(((dec_ref, dec_out), (enc_ref, enc_out), (bias_ref, bias_out)))
    ]
    for copy in copies:
        copy.start()
    for copy in copies:
        copy.wait()


def shards(residual, targets, enc_weight, enc_bias, active, dec_weight, dec_bias, tile_pairs):
    layers, tok, width = residual.shape
    feats = targets.shape[1]
    own = enc_weight.shape[2]
    rows, _, block = dec_weight.shape
    chunk = tok // HALVES
    any_space = pl.BlockSpec(memory_space=pl.ANY)
    vmem = pl.BlockSpec(memory_space=pltpu.VMEM)
    dma = pltpu.SemaphoreType.DMA
    blocks = width // 256
    held = pl.pallas_call(
        kernel,
        out_shape=(
            pltpu.VMEM((rows, feats, block), BF16),
            pltpu.VMEM((layers, width, own), BF16),
            pltpu.VMEM((layers, own), F32),
        ),
        in_specs=[
            any_space, any_space, any_space, vmem, any_space, any_space, vmem,
            pl.BlockSpec(memory_space=pltpu.SMEM),
        ],
        out_specs=(vmem, vmem, vmem),
        scratch_shapes=[
            pltpu.VMEM((layers, blocks, HALVES, chunk, 256), BF16),
            pltpu.VMEM((feats, tok), BF16),
            pltpu.VMEM((layers, width, own), BF16),
            pltpu.VMEM((layers, tok, own), jnp.int32),
            pltpu.VMEM((rows, feats, block), BF16),
            pltpu.VMEM((ITEMS, chunk, block), BF16),
            pltpu.VMEM((HALVES, layers, feats, chunk), F32),
            pltpu.VMEM((HALVES, layers, feats, chunk), BF16),
            pltpu.VMEM((HALVES, 8, feats, 128), BF16),
            pltpu.VMEM((HALVES, layers, feats, chunk), BF16),
            pltpu.VMEM((ITEMS, chunk, block), BF16),
            pltpu.VMEM((ITEMS, chunk, block // 2), BF16),
            pltpu.VMEM((ITEMS, chunk, block // 2), BF16),
            pltpu.VMEM((ITEMS, chunk, own), BF16),
            pltpu.VMEM((ITEMS, 2, chunk // 2, own), BF16),
            pltpu.VMEM((ITEMS, 2, 2, chunk, own), BF16),
            pltpu.VMEM((ITEMS, chunk, own), BF16),
            pltpu.VMEM((ITEMS, chunk, own), BF16),
            pltpu.VMEM((layers, tok, own), BF16),
            pltpu.VMEM((HALVES, chunk, layers * feats), BF16),
            pltpu.SMEM((16,), jnp.int32),
            dma((layers, HALVES)), dma((layers,)), dma((layers,)), dma((16,)), dma,
            dma((ITEMS, 9)), dma((ITEMS, 9)), dma((ITEMS, 9)), dma((ITEMS, 9)),
            dma((HALVES, 8)), dma((HALVES, 8)), dma((HALVES, 8)), dma((HALVES, 8)),
        ],
        compiler_params=pltpu.CompilerParams(
            collective_id=0, has_side_effects=True, vmem_limit_bytes=58000000
        ),
    )(residual, targets, enc_weight, enc_bias, active, dec_weight, dec_bias, tile_pairs.T)
    return pl.pallas_call(
        deliver,
        out_shape=tuple(jax.ShapeDtypeStruct(one.shape, one.dtype) for one in held),
        in_specs=[any_space] * 3,
        out_specs=(any_space,) * 3,
        scratch_shapes=[dma((3,))],
        compiler_params=pltpu.CompilerParams(vmem_limit_bytes=1 << 20),
    )(*held)


def solution(mesh):
    in_specs = (
        P(),
        P(None, "tgt", None),
        P(None, None, ("src", "tgt")),
        P(None, ("src", "tgt")),
        P(None, None, ("src", "tgt")),
        P("src", "tgt", None),
        P(None, "tgt"),
        P("src", None),
    )
    out_specs = (P("src", "tgt", None), P(None, None, ("src", "tgt")), P(None, ("src", "tgt")))
    return jax.shard_map(shards, mesh=mesh, in_specs=in_specs, out_specs=out_specs, check_vma=False)
```
